128 devices in a mesh: leaf: 64 (over z, y_hi, x, core), cols: 2 (over y_lo).
Axes of the slice: x: 4, y: 4 (y_hi: 2, y_lo: 2; y = y_hi * 2 + y_lo), z: 4, core: 2. Of those that a mesh axis runs over, the one named last changes fastest.
Arguments:
- coordinates: float32 [64, 262144], P('cols', 'leaf'), may hold values from -6 to 6
- lengthscale: float32 [64], P('cols'), may hold values from 3 to 12
- tree_order: int32 [64, 4096], P('leaf'), may hold values from 0 to 4095, each once within a row
- probes: bfloat16 [262144, 512], P('leaf', 'cols'), may hold values from -6 to 6
- left_basis: bfloat16 [8, 96, 262144], P(None, None, 'leaf'), may hold values from -0.625 to 0.625
- right_basis: bfloat16 [8, 96, 262144], P(None, None, 'leaf'), may hold values from -6 to 6
Outputs:
- applied: float32 [262144, 512], P('leaf', 'cols')
The draws below stay inside these ranges and needn't reach their ends.
Inputs may be any that keep to these rules, and one draw needn't show every extreme that they name: Each row of tree_order names each of the 4096 points of its block once.
All inputs are finite; a program needn't handle non-finite values.
Results may differ from the reference program's by a relative error of at most 0.0028.
Values sent between devices are 32-bit elements; how exact they have to be, the bound alone decides.
No kernel may reach another device: no remote copies, remote signals or barrier semaphores. Data moves between devices by JAX's collectives and lax.ppermute only.
A program may use at most 128 MiB of HBM per device.

```python
import math
import jax
import jax.numpy as jnp
from jax import lax

DIM = 64
RANK = 96
LEAF = 1024
LEVELS = 8
PTS_DEV = 4096
BLOCKS = 64
POINTS = 262144
PROBES = 512


def block_scale(key, shape, pieces, smallest, high):
    level, own = 1.0, jax.random.fold_in(key, 6)
    for axis_at, shards_of in pieces:
        heights = jnp.exp(jax.random.uniform(jax.random.fold_in(own, axis_at), (shards_of,), jnp.float32, smallest / len(pieces), high / len(pieces)))
        level = level * jnp.repeat(heights, shape[axis_at] // shards_of).reshape([-1 if axis == axis_at else 1 for axis in range(len(shape))])
    return level


def noise(stream_key, dims, width, most, cuts=(), held_as=jnp.bfloat16):
    gain = block_scale(stream_key, dims, cuts, -0.22, 0.18) if cuts else 1.0
    array = jax.random.normal(stream_key, dims, jnp.float32) * width * gain
    return jnp.minimum(jnp.maximum(array, -most), most).astype(held_as)


def setup_inputs(seed: int = 0) -> dict:
    splits = jax.random.split(jax.random.key(seed), 7)
    coordinates = noise(splits[0], (DIM, POINTS), 1.0, 6.0, ((0, 2), (1, 64)), jnp.float32)
    lengthscale = jnp.clip(jnp.exp(math.log(12.0) - 1.3862944 * jax.random.uniform(splits[1], (DIM,), jnp.float32) ** block_scale(splits[1], (DIM,), ((0, 2),), -0.2, 0.2)), 3.0, 12.0)
    tree_order = jax.vmap(lambda own: jax.random.permutation(own, PTS_DEV))(jax.random.split(splits[2], BLOCKS)).reshape((BLOCKS, PTS_DEV)).astype(jnp.int32)
    probes = noise(splits[3], (POINTS, PROBES), 1.0, 6.0, ((0, 64), (1, 2)))
    left_basis = noise(splits[4], (LEVELS, RANK, POINTS), RANK ** -0.5, 0.625, ((2, 64),))
    right_basis = noise(splits[5], (LEVELS, RANK, POINTS), 1.0, 6.0, ((2, 64),))
    return dict(coordinates=coordinates, lengthscale=lengthscale, tree_order=tree_order, probes=probes, left_basis=left_basis, right_basis=right_basis)


def leaf_product(leaf_block):
    scaled, values = leaf_block
    gram_tile = jnp.dot(scaled.T, scaled, precision=lax.Precision.HIGHEST, preferred_element_type=jnp.float32)
    squared = lax.optimization_barrier(jnp.sum(scaled * scaled, axis=0))
    kernel = jnp.exp(-0.5 * (squared[:, None] + squared[None, :] - 2.0 * gram_tile)).astype(jnp.bfloat16)
    return jnp.dot(kernel, values, preferred_element_type=jnp.float32)

def reference(coordinates, lengthscale, tree_order, probes, left_basis, right_basis):
    offsets = (jnp.arange(BLOCKS, dtype=jnp.int32) * PTS_DEV)[:, None]
    source = (tree_order + offsets).reshape(-1).astype(jnp.int32)
    scaled = coordinates[:, source] / lengthscale[:, None]
    values = probes[source]
    leaves = POINTS // LEAF
    blocks = (scaled.reshape(DIM, leaves, LEAF).transpose(1, 0, 2), values.reshape(leaves, LEAF, PROBES))
    result = lax.map(leaf_product, blocks).reshape(POINTS, PROBES)
    wide_values = values.astype(jnp.float32)
    for height in range(1, LEVELS + 1):
        node_count = 2 ** height
        node_size = POINTS // node_count
        right_part = right_basis[height - 1].astype(jnp.float32).reshape(RANK, node_count, node_size)
        coefficient = jnp.einsum('rnm,nmc->nrc', right_part, wide_values.reshape(node_count, node_size, PROBES))
        coefficient = (coefficient * (1.0 / math.sqrt(node_size))).astype(jnp.bfloat16)
        sibling = jnp.flip(coefficient.reshape(node_count // 2, 2, RANK, PROBES), axis=1).reshape(node_count, RANK, PROBES)
        left_part = left_basis[height - 1].astype(jnp.float32).reshape(RANK, node_count, node_size)
        result = result + jnp.einsum('rnm,nrc->nmc', left_part, sibling.astype(jnp.float32)).reshape(POINTS, PROBES)
    return jnp.zeros((POINTS, PROBES), jnp.float32).at[source].set(result)
```

```python
import functools
import math

import jax
import jax.numpy as jnp
from jax import lax
from jax.experimental import pallas as pl
from jax.experimental.pallas import tpu as pltpu
from jax.sharding import PartitionSpec as P

DIM = 64
RANK = 96
LEAF = 1024
CROSS = 6
PTS = 4096
COLS = 256
LEAVES = PTS // LEAF
ROOT = math.sqrt(math.log2(math.e))
F32 = jnp.float32
BF16 = jnp.bfloat16
VM = 64 * 1024 * 1024 - 2 * 1024 * 1024


def whole(shape):
    return pl.BlockSpec(shape, lambda *_: (0,) * len(shape))


def move_rows(order, source, target, width, scatter, unroll=16):
    def group(step, carry):
        for k in range(unroll):
            t = step * unroll + k
            far = order[t]
            near = t
            take, put = (near, far) if scatter else (far, near)
            target[pl.ds(put * width, width), :] = source[pl.ds(take * width, width), :]
        return carry

    lax.fori_loop(0, PTS // unroll, group, 0)


def right_kernel(order, core, probes, right, values, send, keep, coef7, coef8, rows, moved, acc):
    def spread(step, carry):
        base = step * 16
        block = probes[pl.ds(base, 16), :].astype(F32)
        rows[pl.ds(2 * base, 16, stride=2), :] = block[:, :128]
        rows[pl.ds(2 * base + 1, 16, stride=2), :] = block[:, 128:]
        return carry

    lax.fori_loop(0, PTS // 16, spread, 0, unroll=4)
    move_rows(order, rows, moved, 2, False)

    def gather_back(step, carry):
        base = step * 16
        low = moved[pl.ds(2 * base, 16, stride=2), :]
        high = moved[pl.ds(2 * base + 1, 16, stride=2), :]
        values[pl.ds(base, 16), :] = jnp.concatenate([low, high], axis=1).astype(BF16)
        return carry

    lax.fori_loop(0, PTS // 16, gather_back, 0, unroll=4)
    half = []
    for leaf in range(LEAVES):
        span = pl.ds(leaf * LEAF, LEAF)
        part = jnp.dot(
            right[:, :, span].reshape(8 * RANK, LEAF), values[span, :], preferred_element_type=F32
        )
        if leaf == 0:
            acc[...] = part[: CROSS * RANK]
        else:
            acc[...] += part[: CROSS * RANK]
        coef8[leaf] = (part[7 * RANK :] * (1.0 / math.sqrt(LEAF))).astype(BF16)
        half.append(part[6 * RANK : 7 * RANK])
    for node in range(2):
        total = half[2 * node] + half[2 * node + 1]
        coef7[node] = (total * (1.0 / math.sqrt(2 * LEAF))).astype(BF16)

    def level(bit):
        return acc[pl.ds((CROSS - 1 - bit) * RANK, RANK), :]

    send[0] = level(0)

    @pl.when(core[0] == 0)
    def _():
        for k in range(3):
            send[1 + k] = level(1 + k)
        keep[0] = level(4)
        keep[1] = level(5)
        keep[2] = jnp.zeros((RANK, COLS), F32)

    @pl.when(core[0] == 1)
    def _():
        for k in range(3):
            keep[k] = level(1 + k)
        send[1] = level(4)
        send[2] = level(5)
        send[3] = jnp.zeros((RANK, COLS), F32)


def right_stage(order, core, probes, right):
    smem = pl.BlockSpec(memory_space=pltpu.SMEM)
    return pl.pallas_call(
        right_kernel,
        out_shape=(
            jax.ShapeDtypeStruct((PTS, COLS), BF16),
            jax.ShapeDtypeStruct((4, RANK, COLS), F32),
            jax.ShapeDtypeStruct((3, RANK, COLS), F32),
            jax.ShapeDtypeStruct((2, RANK, COLS), BF16),
            jax.ShapeDtypeStruct((4, RANK, COLS), BF16),
        ),
        in_specs=[smem, smem, whole((PTS, COLS)), whole((8, RANK, PTS))],
        out_specs=(
            whole((PTS, COLS)),
            whole((4, RANK, COLS)),
            whole((3, RANK, COLS)),
            whole((2, RANK, COLS)),
            whole((4, RANK, COLS)),
        ),
        scratch_shapes=[
            pltpu.VMEM((2 * PTS, 128), F32),
            pltpu.VMEM((2 * PTS, 128), F32),
            pltpu.VMEM((CROSS * RANK, COLS), F32),
        ],
        compiler_params=pltpu.CompilerParams(vmem_limit_bytes=VM),
        cost_estimate=pl.CostEstimate(
            flops=2 * 768 * PTS * COLS, bytes_accessed=12 << 20, transcendentals=0
        ),
        name="right_stage",
    )(order, core, probes, right)


def points_kernel(order, own, other, left, right, rows, moved):
    def turn(step, carry):
        span = pl.ds(pl.multiple_of(step * 128, 128), 128)
        tile = jnp.concatenate([own[:, span], other[:, span]], axis=0) * ROOT
        rows[span, :] = jnp.concatenate([tile, tile], axis=0).T
        return carry

    lax.fori_loop(0, PTS // 128, turn, 0, unroll=2)
    move_rows(order, rows, moved, 1, False)

    def split(step, carry):
        span = pl.ds(pl.multiple_of(step * 32, 32), 32)
        x = moved[span, :]
        lane = lax.broadcasted_iota(jnp.int32, x.shape, 1)
        high = x.astype(BF16).astype(F32)
        low = x - high
        norm = jnp.sum(x * x, axis=1, keepdims=True) * -0.25
        first = norm.astype(BF16).astype(F32)
        second = (norm - first).astype(BF16).astype(F32)
        third = norm - first - second
        terms = jnp.where(lane % 3 == 0, second, jnp.where(lane % 3 == 1, first, third))
        one = jnp.ones_like(x)
        zero = jnp.zeros_like(x)
        early = lane < 67
        tail = lane < 70
        extra_left = jnp.where(early, terms, jnp.where(tail, one, zero))
        extra_right = jnp.where(early, one, jnp.where(tail, terms, zero))
        front = lane < DIM
        left[span, :] = jnp.concatenate([high, jnp.where(front, low, extra_left)], axis=1).astype(BF16)
        right[span, :] = jnp.concatenate(
            [jnp.where(front, high, low), jnp.where(front, high, extra_right)], axis=1
        ).astype(BF16)
        return carry

    lax.fori_loop(0, PTS // 32, split, 0, unroll=2)


def points_stage(order, own, other):
    return pl.pallas_call(
        points_kernel,
        out_shape=(
            jax.ShapeDtypeStruct((PTS, 256), BF16),
            jax.ShapeDtypeStruct((PTS, 256), BF16),
        ),
        in_specs=[
            pl.BlockSpec(memory_space=pltpu.SMEM),
            whole((DIM // 2, PTS)),
            whole((DIM // 2, PTS)),
        ],
        out_specs=(whole((PTS, 256)), whole((PTS, 256))),
        scratch_shapes=[pltpu.VMEM((PTS, 128), F32), pltpu.VMEM((PTS, 128), F32)],
        compiler_params=pltpu.CompilerParams(vmem_limit_bytes=VM),
        cost_estimate=pl.CostEstimate(flops=PTS * 4096, bytes_accessed=5 << 20, transcendentals=0),
        name="points_stage",
    )(order, own, other)


def near_kernel(left, right, values, basis, coef7, coef8, near):
    leaf = pl.program_id(0)
    block = 256
    coef = jnp.concatenate([coef7[...], coef8[...]], axis=0)
    for step in range(LEAF // block):
        span = pl.ds(step * block, block)
        power = lax.dot_general(
            left[span, :], right[...], (((1,), (1,)), ((), ())), preferred_element_type=F32
        )
        kernel = jnp.exp2(power).astype(BF16)
        total = jnp.dot(kernel, values[...], preferred_element_type=F32)
        total += lax.dot_general(
            basis[:, :, span].reshape(2 * RANK, block),
            coef,
            (((0,), (0,)), ((), ())),
            preferred_element_type=F32,
        )
        near[span, :] = total


def near_stage(left, right, values, basis, coef7, coef8):
    return pl.pallas_call(
        near_kernel,
        grid=(LEAVES,),
        out_shape=jax.ShapeDtypeStruct((PTS, COLS), F32),
        in_specs=[
            pl.BlockSpec((LEAF, 256), lambda i: (i, 0)),
            pl.BlockSpec((LEAF, 256), lambda i: (i, 0)),
            pl.BlockSpec((LEAF, COLS), lambda i: (i, 0)),
            pl.BlockSpec((2, RANK, LEAF), lambda i: (3, 0, i)),
            pl.BlockSpec((None, RANK, COLS), lambda i: (1 - i // 2, 0, 0)),
            pl.BlockSpec((None, RANK, COLS), lambda i: (i + 1 - 2 * (i % 2), 0, 0)),
        ],
        out_specs=pl.BlockSpec((LEAF, COLS), lambda i: (i, 0)),
        compiler_params=pltpu.CompilerParams(vmem_limit_bytes=VM),
        cost_estimate=pl.CostEstimate(
            flops=2 * PTS * LEAF * 512, bytes_accessed=12 << 20, transcendentals=PTS * LEAF
        ),
        name="near_stage",
    )(left, right, values, basis, coef7, coef8)


def finish_kernel(order, core, near, basis, zero, mine, theirs, fourth, fifth, out, coef, rows, moved):
    block = 256
    root = [1.0 / math.sqrt(PTS * 2**bit) for bit in range(CROSS)]

    def put(bit, value):
        coef[pl.ds((CROSS - 1 - bit) * RANK, RANK), :] = (value * root[bit]).astype(BF16)

    put(0, zero[...])

    @pl.when(core[0] == 0)
    def _():
        for k in range(3):
            put(1 + k, theirs[k])
        put(4, mine[0])
        put(5, mine[1])

    @pl.when(core[0] == 1)
    def _():
        for k in range(3):
            put(1 + k, mine[k])
        put(4, fourth[...])
        put(5, fifth[...])

    for step in range(PTS // block):
        span = pl.ds(step * block, block)
        total = near[span, :] + lax.dot_general(
            basis[:, :, span].reshape(CROSS * RANK, block),
            coef[...],
            (((0,), (0,)), ((), ())),
            preferred_element_type=F32,
        )
        rows[pl.ds(2 * step * block, block, stride=2), :] = total[:, :128]
        rows[pl.ds(2 * step * block + 1, block, stride=2), :] = total[:, 128:]
    move_rows(order, rows, moved, 2, True)

    def collect(step, carry):
        base = step * 8
        out[pl.ds(base, 8), :] = jnp.concatenate(
            [moved[pl.ds(2 * base, 8, stride=2), :], moved[pl.ds(2 * base + 1, 8, stride=2), :]], axis=1
        )
        return carry

    lax.fori_loop(0, PTS // 8, collect, 0, unroll=8)


def finish_stage(order, core, near, basis, zero, mine, theirs, fourth, fifth):
    smem = pl.BlockSpec(memory_space=pltpu.SMEM)
    return pl.pallas_call(
        finish_kernel,
        grid=(1,),
        out_shape=jax.ShapeDtypeStruct((PTS, COLS), F32),
        in_specs=[
            smem,
            smem,
            whole((PTS, COLS)),
            whole((CROSS, RANK, PTS)),
            whole((RANK, COLS)),
            whole((3, RANK, COLS)),
            whole((3, RANK, COLS)),
            whole((RANK, COLS)),
            whole((RANK, COLS)),
        ],
        out_specs=whole((PTS, COLS)),
        scratch_shapes=[
            pltpu.VMEM((CROSS * RANK, COLS), BF16),
            pltpu.VMEM((2 * PTS, 128), F32),
            pltpu.VMEM((2 * PTS, 128), F32),
        ],
        compiler_params=pltpu.CompilerParams(vmem_limit_bytes=VM),
        cost_estimate=pl.CostEstimate(
            flops=2 * 576 * PTS * COLS, bytes_accessed=16 << 20, transcendentals=0
        ),
        name="finish_stage",
    )(order, core, near, basis, zero, mine, theirs, fourth, fifth)


def swap(value, masks):
    pairs = []
    for source in range(64):
        mask = masks[source % 2]
        if mask:
            pairs.append((source, source ^ mask))
    return lax.ppermute(value, "leaf", pairs)


CORE, XA, XB, YB, ZA, ZB = 1, 2, 6, 8, 16, 48


def local(coordinates, lengthscale, tree_order, probes, left_basis, right_basis):
    order = tree_order[0]
    side = lax.axis_index("leaf") % 2
    core = side.reshape(1)
    scaled = coordinates / lengthscale[:, None]
    other = lax.ppermute(scaled, "cols", [(0, 1), (1, 0)])
    values, send, keep, coef7, coef8 = right_stage(order, core, probes, right_basis)
    got = swap(send, (CORE, CORE))
    zero = got[0]
    total = keep + got[1:]
    pair = swap(total[:2], (YB, XA))
    lone = swap(total[2], (0, XA))
    first = pair[0]
    pair = total[:2] + pair
    pair = jnp.where(side == 0, pair, jnp.stack([pair[1], total[2] + lone]))
    got = swap(pair, (XA, XB))
    second = got[0]
    pair = pair + got
    got = swap(pair, (XB, YB))
    third = got[1]
    pair = pair + got
    got = swap(pair, (ZA, 0))
    fourth = got[0]
    top = pair[1] + got[1]
    fifth = swap(top, (ZB, 0))
    low = jnp.stack([first, second, third])
    theirs = lax.ppermute(low, "leaf", [(s, s ^ 1) for s in range(64) if s % 2 == 1])
    fourth_in = lax.ppermute(fourth, "leaf", [(s, s ^ 1) for s in range(64) if s % 2 == 0])
    fifth_in = lax.ppermute(fifth, "leaf", [(s, s ^ 1) for s in range(64) if s % 2 == 0])
    mine = jnp.where(side == 0, jnp.stack([fourth, fifth, fifth]), low)
    point_left, point_right = points_stage(order, scaled, other)
    near = near_stage(point_left, point_right, values, left_basis, coef7, coef8)
    return finish_stage(order, core, near, left_basis, zero, mine, theirs, fourth_in, fifth_in)


def solution(mesh):
    placed = (
        P("cols", "leaf"),
        P("cols"),
        P("leaf", None),
        P("leaf", "cols"),
        P(None, None, "leaf"),
        P(None, None, "leaf"),
    )
    return jax.shard_map(
        local, mesh=mesh, in_specs=placed, out_specs=P("leaf", "cols"), check_vma=False
    )
```

```python
import functools
import math

import jax
import jax.numpy as jnp
from jax import lax
from jax.experimental import pallas as pl
from jax.experimental.pallas import tpu as pltpu
from jax.sharding import PartitionSpec as P


DIM = 64
RANK = 96
LEAF = 1024
CROSS = 6
PTS = 4096
COLS = 256
LEAVES = PTS // LEAF
BLOCK = 256
BLOCKS = PTS // BLOCK
ROOT = math.sqrt(math.log2(math.e))
F32 = jnp.float32
BF16 = jnp.bfloat16
LIMIT = 30 * 1024 * 1024
FULL = 60500 * 1024
HALF = RANK // 2
HBM = pl.BlockSpec(memory_space=pltpu.HBM)
VMEM = pl.BlockSpec(memory_space=pltpu.VMEM)
SMEM = pl.BlockSpec(memory_space=pltpu.SMEM)


def call(body, outs, ins, scratch, flops, moved, exps=0, limit=LIMIT):
    return pl.pallas_call(
        body,
        out_shape=tuple(jax.ShapeDtypeStruct(shape, kind) for shape, kind, _ in outs),
        in_specs=ins,
        out_specs=tuple(space for _, _, space in outs),
        scratch_shapes=scratch,
        compiler_params=pltpu.CompilerParams(vmem_limit_bytes=limit),
        cost_estimate=pl.CostEstimate(flops=flops, bytes_accessed=moved, transcendentals=exps),
    )


def right_kernel(order, core, probes, right, values, send, keep, double,
                 raw, table, source, basis, rows, moved, acc, sems):
    get_order = pltpu.make_async_copy(order, raw, sems.at[0])
    get_order.start()
    get_probes = []
    for part in range(4):
        span = pl.ds(part * LEAF, LEAF)
        get_probes.append(pltpu.make_async_copy(probes.at[span], source.at[span], sems.at[1 + part]))
        get_probes[-1].start()
    get_right = []
    for part in range(4):
        span = pl.ds(part * LEAF, LEAF)
        get_right.append(
            pltpu.make_async_copy(
                right.at[pl.ds(0, CROSS), :, span], basis.at[:, :, span], sems.at[5 + part]
            )
        )
        get_right[-1].start()
    get_order.wait()
    double[...] = raw[...] * 2
    get_table = pltpu.make_async_copy(double, table, sems.at[9])
    get_table.start()

    def spread(step, carry):
        base = pl.multiple_of(step * 16, 16)
        block = source[pl.ds(base, 16), :].astype(F32)
        rows[pl.ds(2 * base, 16, stride=2), :] = block[:, :128]
        rows[pl.ds(2 * base + 1, 16, stride=2), :] = block[:, 128:]
        return carry

    for part in range(4):
        get_probes[part].wait()
        lax.fori_loop(part * 64, part * 64 + 64, spread, 0, unroll=8)
    get_table.wait()
    for k in range(PTS):
        moved[pl.ds(2 * k, 2), :] = rows[pl.ds(table[k // 128, k % 128], 2), :]

    def gather_back(step, carry):
        base = pl.multiple_of(step * 64, 64)
        low = moved[pl.ds(2 * base, 64, stride=2), :]
        high = moved[pl.ds(2 * base + 1, 64, stride=2), :]
        values[pl.ds(base, 64), :] = jnp.concatenate([low, high], axis=1).astype(BF16)
        return carry

    lax.fori_loop(0, PTS // 64, gather_back, 0, unroll=4)
    for leaf in range(LEAVES):
        get_right[leaf].wait()
        span = pl.ds(leaf * LEAF, LEAF)
        part = jnp.dot(
            basis[:, :, span].reshape(CROSS * RANK, LEAF), values[span, :], preferred_element_type=F32
        )
        if leaf == 0:
            acc[...] = part
        else:
            acc[...] += part
    send[pl.ds(0, RANK), :] = acc[pl.ds((CROSS - 1) * RANK, RANK), :]
    for bit in range(1, CROSS):
        top = (CROSS - 1 - bit) * RANK
        mine = pl.multiple_of(top + core[0] * HALF, HALF)
        other = pl.multiple_of(top + (1 - core[0]) * HALF, HALF)
        keep[pl.ds((bit - 1) * HALF, HALF), :] = acc[pl.ds(mine, HALF), :]
        send[pl.ds(RANK + (bit - 1) * HALF, HALF), :] = acc[pl.ds(other, HALF), :]


def right_stage(order, core, probes, right):
    return call(
        right_kernel,
        [
            ((PTS, COLS), BF16, VMEM),
            ((RANK + 5 * HALF, COLS), F32, VMEM),
            ((5 * HALF, COLS), F32, VMEM),
            ((32, 128), jnp.int32, VMEM),
        ],
        [HBM, SMEM, HBM, HBM],
        [
            pltpu.VMEM((32, 128), jnp.int32),
            pltpu.SMEM((32, 128), jnp.int32),
            pltpu.VMEM((PTS, COLS), BF16),
            pltpu.VMEM((CROSS, RANK, PTS), BF16),
            pltpu.VMEM((2 * PTS, 128), F32),
            pltpu.VMEM((2 * PTS, 128), F32),
            pltpu.VMEM((CROSS * RANK, COLS), F32),
            pltpu.SemaphoreType.DMA((10,)),
        ],
        2 * 576 * PTS * COLS, 12 << 20, limit=FULL,
    )(order, core, probes, right)


def coef_kernel(right, values, coef7, coef8):
    half = []
    for leaf in range(LEAVES):
        span = pl.ds(leaf * LEAF, LEAF)
        part = jnp.dot(
            right[:, :, span].reshape(2 * RANK, LEAF), values[span, :], preferred_element_type=F32
        )
        coef8[leaf] = (part[RANK:] * (1.0 / math.sqrt(LEAF))).astype(BF16)
        half.append(part[:RANK])
    for node in range(2):
        total = half[2 * node] + half[2 * node + 1]
        coef7[node] = (total * (1.0 / math.sqrt(2 * LEAF))).astype(BF16)


def coef_stage(right, values):
    return call(
        coef_kernel,
        [((2, RANK, COLS), BF16, VMEM), ((4, RANK, COLS), BF16, VMEM)],
        [VMEM, VMEM],
        [],
        2 * 192 * PTS * COLS, 4 << 20,
    )(right, values)


def turn_kernel(own, other, rows):
    line = lax.broadcasted_iota(jnp.int32, (DIM, 128), 0)
    for step in range(PTS // 128):
        span = pl.ds(step * 128, 128)
        tile = jnp.concatenate([own[:, span], other[:, span]], axis=0) * ROOT
        norm = jnp.sum(tile * tile, axis=0, keepdims=True) * -0.5
        first = norm.astype(BF16).astype(F32)
        second = (norm - first).astype(BF16).astype(F32)
        third = norm - first - second
        early = jnp.where(line == 0, first, jnp.where(line == 1, second, third))
        late = jnp.where(line == 3, first, jnp.where(line == 4, second, third))
        extra_left = jnp.where(line < 3, early, jnp.where(line < 6, 1.0, 0.0))
        extra_right = jnp.where(line < 3, 1.0, jnp.where(line < 6, late, 0.0))
        rows[pl.ds(2 * step * 128, 128, stride=2), :] = jnp.concatenate([tile, tile], axis=0).T
        rows[pl.ds(2 * step * 128 + 1, 128, stride=2), :] = jnp.concatenate(
            [extra_right, extra_left], axis=0
        ).T


def turn_stage(own, other):
    return call(
        turn_kernel,
        [((2 * PTS, 128), F32, VMEM)],
        [VMEM, VMEM],
        [],
        PTS * 64, 5 << 20,
    )(own, other)[0]


def points_kernel(half, order, rows, left, right, moved):
    count = BLOCKS // 2

    def gather(block, carry):
        base = pl.multiple_of(block * (2 * BLOCK), 2 * BLOCK)
        for k in range(BLOCK):
            take = order[2 * (block + half * count) + k // 128, k % 128]
            moved[pl.ds(base + 2 * k, 2), :] = rows[pl.ds(take, 2), :]
        return carry

    def split(step, carry):
        base = pl.multiple_of(step * 64, 64)
        span = pl.ds(base, 64)
        x = moved[pl.ds(2 * base, 64, stride=2), :]
        extra = moved[pl.ds(2 * base + 1, 64, stride=2), :]
        front = lax.broadcasted_iota(jnp.int32, x.shape, 1) < DIM
        high = x.astype(BF16).astype(F32)
        low = x - high
        left[span, :] = jnp.concatenate([high, jnp.where(front, low, extra)], axis=1).astype(BF16)
        right[span, :] = jnp.concatenate(
            [jnp.where(front, high, low), jnp.where(front, high, pltpu.roll(extra, DIM, 1))], axis=1
        ).astype(BF16)
        return carry

    lax.fori_loop(0, count, gather, 0)
    lax.fori_loop(0, PTS // 128, split, 0, unroll=2)


def points_stage(half, order, rows):
    return call(
        functools.partial(points_kernel, half),
        [((PTS // 2, 256), BF16, VMEM), ((PTS // 2, 256), BF16, VMEM)],
        [SMEM, VMEM],
        [pltpu.VMEM((PTS, 128), F32)],
        PTS * 2048, 4 << 20,
    )(order, rows)


def near_kernel(leaf, left, right, values, basis, coef7, coef8, near):
    coef = jnp.concatenate([coef7[1 - leaf // 2], coef8[leaf ^ 1]], axis=0)
    local = pl.ds((leaf % 2) * LEAF, LEAF)
    for step in range(LEAF // BLOCK):
        span = pl.ds(step * BLOCK, BLOCK)
        power = lax.dot_general(
            left[pl.ds((leaf % 2) * LEAF + step * BLOCK, BLOCK), :],
            right[local, :],
            (((1,), (1,)), ((), ())),
            preferred_element_type=F32,
        )
        kernel = jnp.exp2(power).astype(BF16)
        total = jnp.dot(kernel, values[pl.ds(leaf * LEAF, LEAF), :], preferred_element_type=F32)
        total += lax.dot_general(
            basis[CROSS:, :, pl.ds(leaf * LEAF + step * BLOCK, BLOCK)].reshape(2 * RANK, BLOCK),
            coef,
            (((0,), (0,)), ((), ())),
            preferred_element_type=F32,
        )
        near[span, :] = total


def near_stage(leaf, left, right, values, basis, coef7, coef8):
    return call(
        functools.partial(near_kernel, leaf),
        [((LEAF, COLS), F32, VMEM)],
        [VMEM] * 6,
        [],
        2 * LEAF * LEAF * 512, 3 << 20, LEAF * LEAF,
    )(left, right, values, basis, coef7, coef8)[0]


def finish_kernel(order, core, near0, near1, near2, near3, basis, zero, first, second, third, fourth,
                  fifth, others, last, out, coef, low, high, moved_low, moved_high, sems):
    root = [1.0 / math.sqrt(PTS * 2**bit) for bit in range(CROSS)]
    near = [near0, near1, near2, near3]
    mine = [first, second, third, fourth, fifth]

    def put(bit, start, value):
        begin = pl.multiple_of((CROSS - 1 - bit) * RANK + start, 16)
        coef[pl.ds(begin, value.shape[0]), :] = (value * root[bit]).astype(BF16)

    put(0, 0, zero[:RANK])
    for bit in range(1, CROSS):
        put(bit, core[0] * HALF, mine[bit - 1][:HALF])
        other = last[...] if bit == 5 else others[pl.ds((bit - 1) * HALF, HALF), :]
        put(bit, (1 - core[0]) * HALF, other)

    for block in range(BLOCKS):
        leaf, step = divmod(block, LEAF // BLOCK)
        span = pl.ds(block * BLOCK, BLOCK)
        total = near[leaf][pl.ds(step * BLOCK, BLOCK), :] + lax.dot_general(
            basis[:CROSS, :, span].reshape(CROSS * RANK, BLOCK),
            coef[...],
            (((0,), (0,)), ((), ())),
            preferred_element_type=F32,
        )
        low[span, :] = total[:, :128]
        high[span, :] = total[:, 128:]

    def scatter(block, carry):
        base = pl.multiple_of(block * 128, 128)
        for k in range(128):
            to = pl.ds(order[block, k], 1)
            moved_low[to, :] = low[pl.ds(base + k, 1), :]
            moved_high[to, :] = high[pl.ds(base + k, 1), :]
        return carry

    lax.fori_loop(0, PTS // 128, scatter, 0)
    copies = []
    for part in range(2):
        moved = (moved_low, moved_high)[part]
        copies.append(
            pltpu.make_async_copy(moved.reshape(PTS // 8, 8, 128), out.at[:, part], sems.at[part])
        )
        copies[-1].start()
    for copy in copies:
        copy.wait()


def finish_stage(order, core, near, basis, coefs):
    out = call(
        finish_kernel,
        [((PTS // 8, 2, 8, 128), F32, HBM)],
        [SMEM, SMEM] + [VMEM] * 13,
        [pltpu.VMEM((CROSS * RANK, COLS), BF16)]
        + [pltpu.VMEM((PTS, 128), F32)] * 4
        + [pltpu.SemaphoreType.DMA((2,))],
        2 * 576 * PTS * COLS, 16 << 20,
    )(order, core, *near, basis, *coefs)[0]
    return out.transpose(0, 2, 1, 3).reshape(PTS, COLS)


CORE, XA, X2, YB, ZA, Z2 = 1, 2, 4, 8, 16, 32


def swap(value, mask):
    pairs = [(source, source ^ mask) for source in range(64)]
    return lax.ppermute(value, "leaf", pairs)


def body(coordinates, lengthscale, tree_order, probes, left_basis, right_basis):
    core = (lax.axis_index("leaf") % 2).reshape(1)
    order = tree_order.reshape(32, 128)
    scaled = coordinates / lengthscale[:, None]
    other = lax.ppermute(scaled, "cols", [(0, 1), (1, 0)])
    values, send, keep, double = right_stage(order, core, probes, right_basis)
    zero = swap(send, CORE)
    total = keep + zero[RANK:]
    first = swap(total, XA)
    total = total[HALF:] + first[HALF:]
    second = swap(total, X2)
    total = total[HALF:] + second[HALF:]
    third = swap(total, YB)
    total = total[HALF:] + third[HALF:]
    fourth = swap(total, ZA)
    total = total[HALF:] + fourth[HALF:]
    fifth = swap(total, Z2)
    ready = jnp.concatenate([first[:HALF], second[:HALF], third[:HALF], fourth[:HALF]])
    others = swap(ready, CORE)
    last = swap(fifth, CORE)
    coef7, coef8 = coef_stage(right_basis[CROSS:], values)
    rows = turn_stage(scaled, other)
    near = []
    for half in range(2):
        left, right = points_stage(half, double, rows)
        for leaf in (2 * half, 2 * half + 1):
            near.append(near_stage(leaf, left, right, values, left_basis, coef7, coef8))
    coefs = (zero, first, second, third, fourth, fifth, others, last)
    return finish_stage(order, core, near, left_basis, coefs)


def solution(mesh):
    placed = (
        P("cols", "leaf"),
        P("cols"),
        P("leaf", None),
        P("leaf", "cols"),
        P(None, None, "leaf"),
        P(None, None, "leaf"),
    )
    return jax.shard_map(
        body, mesh=mesh, in_specs=placed, out_specs=P("leaf", "cols"), check_vma=False
    )
```

```python
import functools
import math

import jax
import jax.numpy as jnp
from jax import lax
from jax.experimental import pallas as pl
from jax.experimental.pallas import tpu as pltpu
from jax.sharding import PartitionSpec as P


DIM = 64
RANK = 96
LEAF = 1024
CROSS = 6
PTS = 4096
COLS = 256
LEAVES = PTS // LEAF
BLOCK = 256
ROOT = math.sqrt(math.log2(math.e))
F32 = jnp.float32
BF16 = jnp.bfloat16
WIDE = 7
DEPTH = 640
HALF = RANK // 2
HBM = pl.BlockSpec(memory_space=pltpu.HBM)
VMEM = pl.BlockSpec(memory_space=pltpu.VMEM)
SMEM = pl.BlockSpec(memory_space=pltpu.SMEM)


def call(body, outs, ins, scratch, flops, moved, exps=0, mib=3):
    return pl.pallas_call(
        body,
        out_shape=tuple(jax.ShapeDtypeStruct(shape, kind) for shape, kind, _ in outs),
        in_specs=ins,
        out_specs=tuple(space for _, _, space in outs),
        scratch_shapes=scratch,
        compiler_params=pltpu.CompilerParams(vmem_limit_bytes=mib << 20),
        cost_estimate=pl.CostEstimate(flops=flops, bytes_accessed=moved, transcendentals=exps),
    )


def right_kernel(order, core, probes, right, values, send, keep, double, wide, inner,
                 raw, table, source, basis, rows, moved, acc, sems):
    get_order = pltpu.make_async_copy(order, raw, sems.at[10])
    get_order.start()
    get_probes = []
    for part in range(4):
        span = pl.ds(part * LEAF, LEAF)
        get_probes.append(pltpu.make_async_copy(probes.at[span], source.at[span], sems.at[part]))
        get_probes[-1].start()
    get_right = []
    for part in range(4):
        span = pl.ds(part * LEAF, LEAF)
        get_right.append(
            pltpu.make_async_copy(
                right.at[pl.ds(0, CROSS), :, span], basis.at[:, :, span], sems.at[5 + part]
            )
        )
        get_right[-1].start()
    get_inner = pltpu.make_async_copy(right.at[pl.ds(CROSS, 2)], inner, sems.at[9])
    get_inner.start()
    get_order.wait()
    double[...] = raw[...] * 2
    wide[...] = raw[...] * WIDE
    get_table = pltpu.make_async_copy(double, table, sems.at[4])
    get_table.start()

    def spread(step, carry):
        base = pl.multiple_of(step * 16, 16)
        block = source[pl.ds(base, 16), :].astype(F32)
        rows[pl.ds(2 * base, 16, stride=2), :] = block[:, :128]
        rows[pl.ds(2 * base + 1, 16, stride=2), :] = block[:, 128:]
        return carry

    for part in range(4):
        get_probes[part].wait()
        lax.fori_loop(part * 64, part * 64 + 64, spread, 0, unroll=8)
    get_table.wait()
    for k in range(PTS):
        moved[pl.ds(2 * k, 2), :] = rows[pl.ds(table[k // 128, k % 128], 2), :]

    def gather_back(step, carry):
        base = pl.multiple_of(step * 64, 64)
        low = moved[pl.ds(2 * base, 64, stride=2), :]
        high = moved[pl.ds(2 * base + 1, 64, stride=2), :]
        values[pl.ds(base, 64), :] = jnp.concatenate([low, high], axis=1).astype(BF16)
        return carry

    lax.fori_loop(0, PTS // 64, gather_back, 0, unroll=4)
    for leaf in range(LEAVES):
        get_right[leaf].wait()
        span = pl.ds(leaf * LEAF, LEAF)
        part = jnp.dot(
            basis[:, :, span].reshape(CROSS * RANK, LEAF), values[span, :], preferred_element_type=F32
        )
        if leaf == 0:
            acc[...] = part
        else:
            acc[...] += part
    get_inner.wait()
    send[pl.ds(0, RANK), :] = acc[pl.ds((CROSS - 1) * RANK, RANK), :]
    for bit in range(1, CROSS):
        top = (CROSS - 1 - bit) * RANK
        mine = pl.multiple_of(top + core[0] * HALF, HALF)
        other = pl.multiple_of(top + (1 - core[0]) * HALF, HALF)
        keep[pl.ds((bit - 1) * HALF, HALF), :] = acc[pl.ds(mine, HALF), :]
        send[pl.ds(RANK + (bit - 1) * HALF, HALF), :] = acc[pl.ds(other, HALF), :]


def right_stage(order, core, probes, right):
    return call(
        right_kernel,
        [
            ((PTS, COLS), BF16, VMEM),
            ((RANK + 5 * HALF, COLS), F32, VMEM),
            ((5 * HALF, COLS), F32, VMEM),
            ((32, 128), jnp.int32, VMEM),
            ((32, 128), jnp.int32, VMEM),
            ((2, RANK, PTS), BF16, VMEM),
        ],
        [HBM, SMEM, HBM, HBM],
        [
            pltpu.VMEM((32, 128), jnp.int32),
            pltpu.SMEM((32, 128), jnp.int32),
            pltpu.VMEM((PTS, COLS), BF16),
            pltpu.VMEM((CROSS, RANK, PTS), BF16),
            pltpu.VMEM((2 * PTS, 128), F32),
            pltpu.VMEM((2 * PTS, 128), F32),
            pltpu.VMEM((CROSS * RANK, COLS), F32),
            pltpu.SemaphoreType.DMA((11,)),
        ],
        2 * 576 * PTS * COLS, 12 << 20, mib=17,
    )(order, core, probes, right)


def coef_kernel(right, values, coef7, coef8):
    half = []
    for leaf in range(LEAVES):
        span = pl.ds(leaf * LEAF, LEAF)
        part = jnp.dot(
            right[:, :, span].reshape(2 * RANK, LEAF), values[span, :], preferred_element_type=F32
        )
        coef8[leaf] = (part[RANK:] * (1.0 / math.sqrt(LEAF))).astype(BF16)
        half.append(part[:RANK])
    for node in range(2):
        total = half[2 * node] + half[2 * node + 1]
        coef7[node] = (total * (1.0 / math.sqrt(2 * LEAF))).astype(BF16)


def coef_stage(right, values):
    return call(
        coef_kernel,
        [((2, RANK, COLS), BF16, VMEM), ((4, RANK, COLS), BF16, VMEM)],
        [VMEM, VMEM],
        [],
        2 * 192 * PTS * COLS, 4 << 20,
    )(right, values)


def turn_kernel(own, other, rows):
    line = lax.broadcasted_iota(jnp.int32, (DIM, 128), 0)
    for step in range(PTS // 128):
        span = pl.ds(step * 128, 128)
        tile = jnp.concatenate([own[:, span], other[:, span]], axis=0) * ROOT
        norm = jnp.sum(tile * tile, axis=0, keepdims=True) * -0.5
        first = norm.astype(BF16).astype(F32)
        second = (norm - first).astype(BF16).astype(F32)
        third = norm - first - second
        early = jnp.where(line == 0, first, jnp.where(line == 1, second, third))
        late = jnp.where(line == 3, first, jnp.where(line == 4, second, third))
        extra_left = jnp.where(line < 3, early, jnp.where(line < 6, 1.0, 0.0))
        extra_right = jnp.where(line < 3, 1.0, jnp.where(line < 6, late, 0.0))
        rows[pl.ds(2 * step * 128, 128, stride=2), :] = jnp.concatenate([tile, tile], axis=0).T
        rows[pl.ds(2 * step * 128 + 1, 128, stride=2), :] = jnp.concatenate(
            [extra_right, extra_left], axis=0
        ).T


def turn_stage(own, other):
    return call(
        turn_kernel,
        [((2 * PTS, 128), F32, VMEM)],
        [VMEM, VMEM],
        [],
        PTS * 64, 5 << 20,
    )(own, other)[0]


def points_kernel(half, order, rows, left, right, moved):
    for k in range(PTS // 2):
        take = order[half * 16 + k // 128, k % 128]
        moved[pl.ds(2 * k, 2), :] = rows[pl.ds(take, 2), :]

    def split(step, carry):
        base = pl.multiple_of(step * 64, 64)
        span = pl.ds(base, 64)
        x = moved[pl.ds(2 * base, 64, stride=2), :]
        extra = moved[pl.ds(2 * base + 1, 64, stride=2), :]
        front = lax.broadcasted_iota(jnp.int32, x.shape, 1) < DIM
        high = x.astype(BF16).astype(F32)
        low = x - high
        left[span, :] = jnp.concatenate([high, jnp.where(front, low, extra)], axis=1).astype(BF16)
        right[span, :] = jnp.concatenate(
            [jnp.where(front, high, low), jnp.where(front, high, pltpu.roll(extra, DIM, 1))], axis=1
        ).astype(BF16)
        return carry

    lax.fori_loop(0, PTS // 128, split, 0, unroll=2)


def points_stage(half, order, rows):
    return call(
        functools.partial(points_kernel, half),
        [((PTS // 2, 256), BF16, VMEM), ((PTS // 2, 256), BF16, VMEM)],
        [SMEM, VMEM],
        [pltpu.VMEM((PTS, 128), F32)],
        PTS * 2048, 4 << 20, mib=4,
    )(order, rows)


def near_kernel(leaf, left, right, values, basis, coef7, coef8, near):
    coef = jnp.concatenate([coef7[1 - leaf // 2], coef8[leaf ^ 1]], axis=0)
    local = pl.ds((leaf % 2) * LEAF, LEAF)
    for step in range(LEAF // BLOCK):
        power = lax.dot_general(
            left[pl.ds((leaf % 2) * LEAF + step * BLOCK, BLOCK), :],
            right[local, :],
            (((1,), (1,)), ((), ())),
            preferred_element_type=F32,
        )
        kernel = jnp.exp2(power).astype(BF16)
        total = jnp.dot(kernel, values[pl.ds(leaf * LEAF, LEAF), :], preferred_element_type=F32)
        total += lax.dot_general(
            basis[CROSS:, :, pl.ds(leaf * LEAF + step * BLOCK, BLOCK)].reshape(2 * RANK, BLOCK),
            coef,
            (((0,), (0,)), ((), ())),
            preferred_element_type=F32,
        )
        place = WIDE * step * BLOCK
        near[pl.ds(place, BLOCK, stride=WIDE), :] = total[:, :128]
        near[pl.ds(place + 1, BLOCK, stride=WIDE), :] = total[:, 128:]
        turned = basis[:CROSS, :, pl.ds(leaf * LEAF + step * BLOCK, BLOCK)]
        turned = turned.reshape(CROSS * RANK, BLOCK).T.astype(F32)
        turned = jnp.concatenate([turned, jnp.zeros((BLOCK, DEPTH - CROSS * RANK), F32)], axis=1)
        for part in range(DEPTH // 128):
            near[pl.ds(place + 2 + part, BLOCK, stride=WIDE), :] = turned[:, part * 128 : part * 128 + 128]


def near_stage(leaf, left, right, values, basis, coef7, coef8):
    return call(
        functools.partial(near_kernel, leaf),
        [((LEAF * WIDE, 128), F32, VMEM)],
        [VMEM] * 6,
        [],
        2 * LEAF * LEAF * 512, 3 << 20, LEAF * LEAF, mib=6,
    )(left, right, values, basis, coef7, coef8)[0]


def scatter_kernel(order, near0, near1, near2, near3, moved):
    for leaf, near in enumerate((near0, near1, near2, near3)):
        for k in range(LEAF):
            to = order[8 * leaf + k // 128, k % 128]
            moved[pl.ds(to, WIDE), :] = near[pl.ds(WIDE * k, WIDE), :]


def scatter_stage(order, near):
    return call(
        scatter_kernel,
        [((PTS * WIDE, 128), F32, VMEM)],
        [SMEM] + [VMEM] * 4,
        [],
        PTS * 256, 28 << 20,
    )(order, *near)[0]


def collect_kernel(moved, near, turned):
    def collect(step, carry):
        base = pl.multiple_of(step * 64, 64)
        span = pl.ds(base, 64)
        parts = [moved[pl.ds(WIDE * base + k, 64, stride=WIDE), :] for k in range(WIDE)]
        near[span, :] = jnp.concatenate(parts[:2], axis=1)
        turned[span, :] = jnp.concatenate(parts[2:], axis=1).astype(BF16)
        return carry

    lax.fori_loop(0, PTS // 64, collect, 0, unroll=2)


def collect_stage(moved):
    return call(
        collect_kernel,
        [((PTS, COLS), F32, VMEM), ((PTS, DEPTH), BF16, VMEM)],
        [VMEM],
        [],
        PTS * 1024, 24 << 20,
    )(moved)


def finish_kernel(core, near, turned, zero, first, second, third, fourth, fifth, others, last, out,
                  coef, whole, sems):
    root = [1.0 / math.sqrt(PTS * 2**bit) for bit in range(CROSS)]
    mine = [first, second, third, fourth, fifth]

    def put(bit, start, value):
        begin = pl.multiple_of((CROSS - 1 - bit) * RANK + start, 16)
        coef[pl.ds(begin, value.shape[0]), :] = (value * root[bit]).astype(BF16)

    coef[pl.ds(CROSS * RANK, DEPTH - CROSS * RANK), :] = jnp.zeros(
        (DEPTH - CROSS * RANK, COLS), BF16
    )
    put(0, 0, zero[:RANK])
    for bit in range(1, CROSS):
        put(bit, core[0] * HALF, mine[bit - 1][:HALF])
        other = last[...] if bit == 5 else others[pl.ds((bit - 1) * HALF, HALF), :]
        put(bit, (1 - core[0]) * HALF, other)
    copies = []
    for part in range(8):
        span = pl.ds(part * (PTS // 8), PTS // 8)
        whole[span, :] = near[span, :] + jnp.dot(
            turned[span, :], coef[...], preferred_element_type=F32
        )
        copies.append(pltpu.make_async_copy(whole.at[span], out.at[span], sems.at[part]))
        copies[-1].start()
    for copy in copies:
        copy.wait()


def finish_stage(core, near, turned, coefs):
    return call(
        finish_kernel,
        [((PTS, COLS), F32, HBM)],
        [SMEM] + [VMEM] * 10,
        [
            pltpu.VMEM((DEPTH, COLS), BF16),
            pltpu.VMEM((PTS, COLS), F32),
            pltpu.SemaphoreType.DMA((8,)),
        ],
        2 * 576 * PTS * COLS, 8 << 20, mib=8,
    )(core, near, turned, *coefs)[0]


CORE, XA, X2, YB, ZA, Z2 = 1, 2, 4, 8, 16, 32


def swap(value, mask):
    pairs = [(source, source ^ mask) for source in range(64)]
    return lax.ppermute(value, "leaf", pairs)


def body(coordinates, lengthscale, tree_order, probes, left_basis, right_basis):
    core = (lax.axis_index("leaf") % 2).reshape(1)
    order = tree_order.reshape(32, 128)
    scaled = coordinates / lengthscale[:, None]
    other = lax.ppermute(scaled, "cols", [(0, 1), (1, 0)])
    values, send, keep, double, wide, inner = right_stage(
        pltpu.with_memory_space_constraint(order, pltpu.HBM),
        core,
        pltpu.with_memory_space_constraint(probes, pltpu.HBM),
        pltpu.with_memory_space_constraint(right_basis, pltpu.HBM),
    )
    zero = swap(send, CORE)
    total = keep + zero[RANK:]
    first = swap(total, XA)
    total = total[HALF:] + first[HALF:]
    second = swap(total, X2)
    total = total[HALF:] + second[HALF:]
    third = swap(total, YB)
    total = total[HALF:] + third[HALF:]
    fourth = swap(total, ZA)
    total = total[HALF:] + fourth[HALF:]
    fifth = swap(total, Z2)
    ready = jnp.concatenate([first[:HALF], second[:HALF], third[:HALF], fourth[:HALF]])
    others = swap(ready, CORE)
    last = swap(fifth, CORE)
    coef7, coef8 = coef_stage(inner, values)
    rows = turn_stage(scaled, other)
    near = []
    for half in range(2):
        left, right = points_stage(half, double, rows)
        for leaf in (2 * half, 2 * half + 1):
            near.append(near_stage(leaf, left, right, values, left_basis, coef7, coef8))
    coefs = (zero, first, second, third, fourth, fifth, others, last)
    near, turned = collect_stage(scatter_stage(wide, near))
    return finish_stage(core, near, turned, coefs)


def solution(mesh):
    placed = (
        P("cols", "leaf"),
        P("cols"),
        P("leaf", None),
        P("leaf", "cols"),
        P(None, None, "leaf"),
        P(None, None, "leaf"),
    )
    return jax.shard_map(
        body, mesh=mesh, in_specs=placed, out_specs=P("leaf", "cols"), check_vma=False
    )
```
